512 devices in a mesh: dp: 64 (over z_lo, y, x), tensor: 8 (over z_hi, core).
Axes of the slice: x: 4, y: 8, z: 8 (z_hi: 4, z_lo: 2; z = z_hi * 2 + z_lo), core: 2. Of those that a mesh axis runs over, the one named last changes fastest.
Arguments:
- tokens: bfloat16 [8192, 6144], P('dp', 'tensor'), may hold values from -6 to 6
- cotangent: bfloat16 [8192, 6144], P('dp', 'tensor'), may hold values from -6 to 6
- w_gate: bfloat16 [1, 6144, 16384], P(None, 'tensor', 'dp'), may hold values from -0.078125 to 0.078125
- w_up: bfloat16 [1, 6144, 16384], P(None, 'tensor', 'dp'), may hold values from -0.078125 to 0.078125
- w_down: bfloat16 [1, 16384, 6144], P(None, 'dp', 'tensor'), may hold values from -0.046875 to 0.046875
- slot_token: int32 [64, 1, 6], P('dp'), may hold values from -1 to 127, as said below
- route_weight: float32 [64, 1, 6], P('dp'), may hold values from 0.2 to 1
Outputs:
- mixed: bfloat16 [8192, 6144], P('dp', 'tensor')
- grad_tokens: bfloat16 [8192, 6144], P('dp', 'tensor')
- grad_gate: bfloat16 [1, 6144, 16384], P(None, 'tensor', 'dp')
- grad_up: bfloat16 [1, 6144, 16384], P(None, 'tensor', 'dp')
- grad_down: bfloat16 [1, 16384, 6144], P(None, 'dp', 'tensor')
The draws below stay inside these ranges and needn't reach their ends.
Inputs may be any that keep to these rules, and one draw needn't show every extreme that they name: `slot_token`: for each block and expert the filled slots come first and name distinct tokens of that block; every block has at least one filled slot for each expert, and for each expert some block fills all 6 slots.
All inputs are finite; a program needn't handle non-finite values.
Results may differ from the reference program's by a relative error of at most 0.0057.
Values may be sent and summed in bfloat16 or wider, within the bound.
No kernel may reach another device: no remote copies, remote signals or barrier semaphores. Data moves between devices by JAX's collectives and lax.ppermute only.
A program may use at most 64 MiB of HBM per device.

```python
import jax
import jax.numpy as jnp

D = 6144
FF = 16384
E_WIN = 1
TOK_DEV = 128
CAP = 6
DP_BLOCKS = 64
TOKENS = 8192


def first_slots(order_key):
    return jax.random.permutation(order_key, TOK_DEV)[:CAP]


def draw_slot_token(key, part):
    count_key, busiest_key, order_key = jax.random.split(jax.random.fold_in(key, 11), 3)
    counts = jax.random.randint(count_key, (DP_BLOCKS, E_WIN), 1, CAP + 1)
    busiest = jax.random.randint(busiest_key, (E_WIN,), 0, DP_BLOCKS)
    counts = jnp.where(jnp.arange(DP_BLOCKS)[:, None] == busiest[None, :], CAP, counts)
    order_keys = jax.random.split(order_key, DP_BLOCKS * E_WIN)
    orders = jax.vmap(first_slots)(order_keys).reshape(DP_BLOCKS, E_WIN, CAP)
    position = jnp.arange(CAP)[None, None, :]
    return jnp.where(position < counts[:, :, None], orders, -1).astype(jnp.int32)


def shard_levels(stream_key, shape, pieces, least, top_value):
    gain, own = 1.0, jax.random.fold_in(stream_key, 6)
    for axis_at, parts in pieces:
        heights = jnp.exp(jax.random.uniform(jax.random.fold_in(own, axis_at), (parts,), jnp.float32, least / len(pieces), top_value / len(pieces)))
        gain = gain * jnp.repeat(heights, shape[axis_at] // parts).reshape([-1 if axis == axis_at else 1 for axis in range(len(shape))])
    return gain


def normal_values(own_key, dims, spread, reach, cuts=(), kind=jnp.bfloat16):
    values = jax.random.normal(own_key, dims, jnp.float32) * spread
    if len(cuts) > 0:
        values = shard_levels(own_key, dims, cuts, -0.22, 0.18) * values
    return jnp.clip(values, min=-reach, max=reach).astype(kind)


def setup_inputs(seed: int = 0) -> dict:
    splits = jax.random.split(jax.random.key(seed), 8)
    return {
        "tokens": normal_values(splits[0], (TOKENS, D), 1.0, 6.0, ((0, 64), (1, 8))),
        "cotangent": normal_values(splits[1], (TOKENS, D), 1.0, 6.0, ((0, 64), (1, 8))),
        "w_gate": normal_values(splits[2], (E_WIN, D, FF), D ** -0.5, 0.078125, ((1, 8), (2, 64))),
        "w_up": normal_values(splits[3], (E_WIN, D, FF), D ** -0.5, 0.078125, ((1, 8), (2, 64))),
        "w_down": normal_values(splits[4], (E_WIN, FF, D), FF ** -0.5, 0.046875, ((1, 64), (2, 8))),
        "slot_token": draw_slot_token(jax.random.fold_in(splits[7], 71), 0),
        "route_weight": jnp.clip(0.2 + 0.8 * jax.random.uniform(splits[6], (DP_BLOCKS, E_WIN, CAP), jnp.float32) ** shard_levels(splits[6], (DP_BLOCKS, E_WIN, CAP), ((0, 64),), -0.2, 0.2), 0.2, 1.0),
    }


def reference(tokens, cotangent, w_gate, w_up, w_down, slot_token, route_weight):
    blocks = slot_token.shape[0]
    usable = slot_token >= 0
    offsets = (jnp.arange(blocks, dtype=jnp.int32) * TOK_DEV)[:, None, None]
    global_index = jnp.where(usable, slot_token + offsets, 0).astype(jnp.int32)
    segment_index = jnp.where(usable, global_index, TOKENS).astype(jnp.int32)
    mixed = jnp.zeros((TOKENS, D), jnp.float32)
    grad_tokens = jnp.zeros((TOKENS, D), jnp.float32)
    gate_grads = []
    up_grads = []
    down_grads = []
    for expert in range(E_WIN):
        row_index = global_index[:, expert, :].reshape(-1)
        keep_rows = usable[:, expert, :].reshape(-1, 1)
        segments = segment_index[:, expert, :].reshape(-1)
        weights = route_weight[:, expert, :].reshape(-1, 1)
        picked = jnp.where(keep_rows, tokens[row_index], 0).astype(jnp.bfloat16)
        d_rows = (weights * cotangent[row_index].astype(jnp.float32) * keep_rows.astype(jnp.float32)).astype(jnp.bfloat16)
        gate_sum = jnp.dot(picked, w_gate[expert], preferred_element_type=jnp.float32)
        up_sum = jnp.dot(picked, w_up[expert], preferred_element_type=jnp.float32)
        sigmoid_gate = jax.nn.sigmoid(gate_sum)
        activated = gate_sum * sigmoid_gate
        hidden = (activated * up_sum).astype(jnp.bfloat16)
        expert_out = jnp.dot(hidden, w_down[expert], preferred_element_type=jnp.float32)
        mixed = mixed + jax.ops.segment_sum(weights * expert_out, segments, num_segments=TOKENS)
        hidden_grad = jnp.dot(d_rows, w_down[expert].T, preferred_element_type=jnp.float32)
        d_gate = (hidden_grad * up_sum * sigmoid_gate * (1.0 + gate_sum * (1.0 - sigmoid_gate))).astype(jnp.bfloat16)
        d_up = (hidden_grad * activated).astype(jnp.bfloat16)
        down_grads.append(jnp.dot(hidden.T, d_rows, preferred_element_type=jnp.float32).astype(jnp.bfloat16))
        gate_grads.append(jnp.dot(picked.T, d_gate, preferred_element_type=jnp.float32).astype(jnp.bfloat16))
        up_grads.append(jnp.dot(picked.T, d_up, preferred_element_type=jnp.float32).astype(jnp.bfloat16))
        slot_grad = jnp.dot(d_gate, w_gate[expert].T, preferred_element_type=jnp.float32) + jnp.dot(d_up, w_up[expert].T, preferred_element_type=jnp.float32)
        grad_tokens = grad_tokens + jax.ops.segment_sum(slot_grad, segments, num_segments=TOKENS)
    return (mixed.astype(jnp.bfloat16), grad_tokens.astype(jnp.bfloat16), jnp.stack(gate_grads), jnp.stack(up_grads), jnp.stack(down_grads))
```

```python
import jax
import jax.numpy as jnp
from jax import lax
from jax.sharding import Mesh
from jax.sharding import PartitionSpec as P

AXES = ("zl", "y", "x", "zh", "c")
SIZES = (2, 8, 4, 4, 2)
DP = ("zl", "y", "x")
TENSOR = ("zh", "c")
BF16 = jnp.bfloat16
F32 = jnp.float32


def exchange(pieces, axes):
    return lax.all_to_all(pieces, axes, split_axis=0, concat_axis=0, tiled=True)


def spread(piece, axes, n):
    return exchange(jnp.broadcast_to(piece[None], (n, *piece.shape)), axes)


def dot(a, b, ca, cb):
    return lax.dot_general(a, b, (((ca,), (cb,)), ((), ())), preferred_element_type=F32)


def on_device(tokens, cotangent, w_gate, w_up, w_down, slot_token, route_weight):
    w_gate, w_up, w_down = w_gate[0], w_up[0], w_down[0]
    slots, weights = slot_token[0, 0], route_weight[0, 0]
    tok, d = tokens.shape
    cap = slots.shape[0]
    ff = w_gate.shape[1]
    one_hot = (slots[:, None] == jnp.arange(tok, dtype=jnp.int32)[None, :]).astype(BF16)
    picked = dot(one_hot, tokens, 1, 0).astype(BF16)
    d_rows = (weights[:, None] * dot(one_hot, cotangent, 1, 0)).astype(BF16)

    near = spread(jnp.concatenate([picked, d_rows]), "y", 8)
    near = near.reshape(8, 2, cap, d).transpose(1, 0, 2, 3).reshape(2, 8 * cap, d)
    rows = spread(near, ("zl", "x"), 8)
    n = 64 * cap
    all_rows = rows[:, 0].reshape(n, d)
    all_grads = rows[:, 1].reshape(n, d)

    part = jnp.concatenate(
        [dot(all_rows, w_gate, 1, 0), dot(all_rows, w_up, 1, 0), dot(all_grads, w_down, 1, 1)], axis=1
    )
    part = jnp.sum(exchange(part.reshape(2, n // 2, 3 * ff), "c"), axis=0).astype(BF16)
    sums = jnp.sum(exchange(part.reshape(4, n // 8, 3 * ff), "zh").astype(F32), axis=0)
    gate_sum, up_sum, hidden_grad = sums[:, :ff], sums[:, ff : 2 * ff], sums[:, 2 * ff :]
    sigmoid_gate = jax.nn.sigmoid(gate_sum)
    activated = gate_sum * sigmoid_gate
    own = jnp.concatenate(
        [
            activated * up_sum,
            hidden_grad * up_sum * sigmoid_gate * (1.0 + gate_sum * (1.0 - sigmoid_gate)),
            hidden_grad * activated,
        ],
        axis=1,
    ).astype(BF16)
    full = spread(spread(own, "zh", 4).reshape(n // 2, 3 * ff), "c", 2).reshape(n, 3 * ff)
    hidden, d_gate, d_up = full[:, :ff], full[:, ff : 2 * ff], full[:, 2 * ff :]

    out = dot(hidden, w_down, 1, 0).astype(BF16)
    back = (dot(d_gate, w_gate, 1, 1) + dot(d_up, w_up, 1, 1)).astype(BF16)
    both = jnp.stack([out.reshape(8, 8 * cap, d), back.reshape(8, 8 * cap, d)], axis=1)
    both = jnp.sum(exchange(both, ("zl", "x")).astype(F32), axis=0).astype(BF16)
    both = both.reshape(2, 8, cap, d).transpose(1, 0, 2, 3).reshape(8, 2 * cap, d)
    both = jnp.sum(exchange(both, "y").astype(F32), axis=0)
    mixed = dot(one_hot, (weights[:, None] * both[:cap]).astype(BF16), 0, 0).astype(BF16)
    grad_tokens = dot(one_hot, both[cap:].astype(BF16), 0, 0).astype(BF16)

    grad_gate = dot(all_rows, d_gate, 0, 0).astype(BF16)
    grad_up = dot(all_rows, d_up, 0, 0).astype(BF16)
    grad_down = dot(hidden, all_grads, 0, 0).astype(BF16)
    return mixed, grad_tokens, grad_gate[None], grad_up[None], grad_down[None]


def solution(mesh):
    fine = Mesh(mesh.devices.reshape(SIZES), AXES)
    acts = P(DP, TENSOR)
    w_in = P(None, TENSOR, DP)
    w_out = P(None, DP, TENSOR)
    slot = P(DP, None, None)
    return jax.shard_map(
        on_device,
        mesh=fine,
        in_specs=(acts, acts, w_in, w_in, w_out, slot, slot),
        out_specs=(acts, acts, w_in, w_in, w_out),
        check_vma=False,
    )
```

```python
import jax
import jax.numpy as jnp
from jax import lax
from jax.sharding import Mesh
from jax.sharding import PartitionSpec as P

AXES = ("zl", "y", "x", "zh", "c")
SIZES = (2, 8, 4, 4, 2)
DP = ("zl", "y", "x")
TENSOR = ("zh", "c")
BF16 = jnp.bfloat16
F32 = jnp.float32


def exchange(pieces, axes):
    return lax.all_to_all(pieces, axes, split_axis=0, concat_axis=0, tiled=True)


def spread(piece, axes, n):
    return exchange(jnp.broadcast_to(piece[None], (n, *piece.shape)), axes)


def total(pieces):
    out = pieces[0].astype(F32)
    for j in range(1, pieces.shape[0]):
        out = out + pieces[j].astype(F32)
    return out


def dot(a, b, ca, cb):
    return lax.dot_general(a, b, (((ca,), (cb,)), ((), ())), preferred_element_type=F32)


def on_device(tokens, cotangent, w_gate, w_up, w_down, slot_token, route_weight):
    w_gate, w_up, w_down = w_gate[0], w_up[0], w_down[0]
    slots, weights = slot_token[0, 0], route_weight[0, 0]
    tok, d = tokens.shape
    cap = slots.shape[0]
    ff = w_gate.shape[1]
    one_hot = (slots[:, None] == jnp.arange(tok, dtype=jnp.int32)[None, :]).astype(BF16)
    picked = dot(one_hot, tokens, 1, 0).astype(BF16)
    d_rows = (weights[:, None] * dot(one_hot, cotangent, 1, 0)).astype(BF16)

    half = ff // 2
    kept_at = lax.axis_index("c").astype(jnp.uint32) * half
    sent_at = half - kept_at
    near, kept_at, sent_at = lax.optimization_barrier((jnp.concatenate([picked, d_rows]), kept_at, sent_at))
    near = spread(near, "y", 8)
    near = near.reshape(8, 2, cap, d).transpose(1, 0, 2, 3).reshape(2, 8 * cap, d)
    rows = spread(near, ("zl", "x"), 8)
    n = 64 * cap
    all_rows = rows[:, 0].reshape(n, d)
    all_grads = rows[:, 1].reshape(n, d)

    part = jnp.stack([dot(w_gate, all_rows, 0, 1), dot(w_up, all_rows, 0, 1), dot(w_down, all_grads, 1, 1)])
    sent = lax.ppermute(
        lax.dynamic_slice_in_dim(part, sent_at, half, axis=1), "c", [(0, 1), (1, 0)]
    )
    part = (lax.dynamic_slice_in_dim(part, kept_at, half, axis=1) + sent).astype(BF16)
    part = part.reshape(3, 4, ff // 8, n).transpose(1, 0, 2, 3)
    gate_sum, up_sum, hidden_grad = total(exchange(part, "zh"))
    sigmoid_gate = jax.nn.sigmoid(gate_sum)
    activated = gate_sum * sigmoid_gate
    own = jnp.stack(
        [
            activated * up_sum,
            hidden_grad * up_sum * sigmoid_gate * (1.0 + gate_sum * (1.0 - sigmoid_gate)),
            hidden_grad * activated,
        ]
    ).astype(BF16)
    full = lax.all_gather(spread(own, "zh", 4), "c", axis=0, tiled=True)
    hidden, d_gate, d_up = (full[:, i].reshape(ff, n) for i in range(3))

    out = dot(hidden, w_down, 0, 0).astype(BF16)
    back = (dot(d_gate, w_gate, 0, 1) + dot(d_up, w_up, 0, 1)).astype(BF16)
    both = jnp.stack([out.reshape(8, 8 * cap, d), back.reshape(8, 8 * cap, d)], axis=1)
    both = total(exchange(both, ("zl", "x"))).astype(BF16)
    both = both.reshape(2, 8, cap, d).transpose(1, 0, 2, 3).reshape(8, 2 * cap, d)
    both = total(exchange(both, "y"))
    mixed = dot(one_hot, (weights[:, None] * both[:cap]).astype(BF16), 0, 0).astype(BF16)
    grad_tokens = dot(one_hot, both[cap:].astype(BF16), 0, 0).astype(BF16)

    grad_gate = dot(all_rows, d_gate, 0, 1).astype(BF16)
    grad_up = dot(all_rows, d_up, 0, 1).astype(BF16)
    grad_down = dot(hidden, all_grads, 1, 0).astype(BF16)
    return mixed, grad_tokens, grad_gate[None], grad_up[None], grad_down[None]


def solution(mesh):
    fine = Mesh(mesh.devices.reshape(SIZES), AXES)
    acts = P(DP, TENSOR)
    w_in = P(None, TENSOR, DP)
    w_out = P(None, DP, TENSOR)
    slot = P(DP, None, None)
    return jax.shard_map(
        on_device,
        mesh=fine,
        in_specs=(acts, acts, w_in, w_in, w_out, slot, slot),
        out_specs=(acts, acts, w_in, w_in, w_out),
        check_vma=False,
    )
```

```python
import jax
import jax.numpy as jnp
from jax import lax
from jax.experimental import pallas as pl
from jax.experimental.pallas import tpu as pltpu
from jax.sharding import Mesh
from jax.sharding import PartitionSpec as P

AXES = ("zl", "y", "x", "zh", "c")
SIZES = (2, 8, 4, 4, 2)
DP = ("zl", "y", "x")
TENSOR = ("zh", "c")
BF16 = jnp.bfloat16
F32 = jnp.float32


def exchange(pieces, axes):
    return lax.all_to_all(pieces, axes, split_axis=0, concat_axis=0, tiled=True)


def spread(piece, axes, n):
    return exchange(jnp.broadcast_to(piece[None], (n, *piece.shape)), axes)


def total(pieces):
    out = pieces[0].astype(F32)
    for j in range(1, pieces.shape[0]):
        out = out + pieces[j].astype(F32)
    return out


def dot(a, b, ca, cb):
    return lax.dot_general(a, b, (((ca,), (cb,)), ((), ())), preferred_element_type=F32)


def one_hot(slots_ref, shape, slot_dim, first):
    slot = lax.broadcasted_iota(jnp.int32, shape, slot_dim) - first
    token = lax.broadcasted_iota(jnp.int32, shape, 1 - slot_dim)
    wanted = jnp.full(shape, -1, jnp.int32)
    for s in range(slots_ref.shape[0]):
        wanted = jnp.where(slot == s, slots_ref[s], wanted)
    return (token == wanted).astype(F32).astype(BF16)


def by_slot(weights_ref, rows, first, other):
    slot = lax.broadcasted_iota(jnp.int32, (rows, 1), 0) - first
    out = jnp.full((rows, 1), other, F32)
    for s in range(weights_ref.shape[0]):
        out = jnp.where(slot == s, weights_ref[s], out)
    return out


def pick_body(slots_ref, weights_ref, tokens_ref, cotangent_ref, out_ref):
    cap = slots_ref.shape[0]
    copies, rows, _ = out_ref.shape
    hot = one_hot(slots_ref, (rows, tokens_ref.shape[0]), 0, 0)
    hot_d = one_hot(slots_ref, (rows, tokens_ref.shape[0]), 0, cap)
    picked = dot(hot, tokens_ref[...], 1, 0)
    d_rows = by_slot(weights_ref, rows, cap, 0.0) * dot(hot_d, cotangent_ref[...], 1, 0)
    packed = (picked + d_rows).astype(BF16)
    for j in range(copies):
        out_ref[j] = packed


def place_body(slots_ref, weights_ref, pieces_ref, mixed_ref, grad_ref):
    cap = slots_ref.shape[0]
    copies, rows, _ = pieces_ref.shape
    tok = mixed_ref.shape[0]
    acc = pieces_ref[0].astype(F32)
    for j in range(1, copies):
        acc = acc + pieces_ref[j].astype(F32)
    acc = (acc * by_slot(weights_ref, rows, 0, 1.0)).astype(BF16)
    mixed_ref[...] = dot(one_hot(slots_ref, (tok, rows), 1, 0), acc, 1, 0).astype(BF16)
    grad_ref[...] = dot(one_hot(slots_ref, (tok, rows), 1, cap), acc, 1, 0).astype(BF16)


SMEM = pl.BlockSpec(memory_space=pltpu.SMEM)
VMEM = pl.BlockSpec(memory_space=pltpu.VMEM)


def pick(slots, weights, tokens, cotangent, copies):
    return pl.pallas_call(
        pick_body,
        in_specs=[SMEM, SMEM, VMEM, VMEM],
        out_specs=VMEM,
        out_shape=pltpu.VMEM((copies, 2 * slots.shape[0], tokens.shape[1]), BF16),
    )(slots, weights, tokens, cotangent)


def place(slots, weights, pieces, tok):
    out = jax.ShapeDtypeStruct((tok, pieces.shape[2]), BF16)
    return pl.pallas_call(
        place_body, in_specs=[SMEM, SMEM, VMEM], out_specs=(VMEM, VMEM), out_shape=(out, out)
    )(slots, weights, pltpu.with_memory_space_constraint(pieces, pltpu.VMEM))


def on_device(tokens, cotangent, w_gate, w_up, w_down, slot_token, route_weight):
    w_gate, w_up, w_down = w_gate[0], w_up[0], w_down[0]
    slots, weights = slot_token[0, 0], route_weight[0, 0]
    tok, d = tokens.shape
    cap = slots.shape[0]
    ff = w_gate.shape[1]

    half = ff // 2
    kept_at = lax.axis_index("c").astype(jnp.uint32) * half
    sent_at = half - kept_at
    near, kept_at, sent_at = lax.optimization_barrier(
        (pick(slots, weights, tokens, cotangent, 8), kept_at, sent_at)
    )
    near = exchange(near, "y")
    near = near.reshape(8, 2, cap, d).transpose(1, 0, 2, 3).reshape(2, 8 * cap, d)
    rows = spread(near, ("zl", "x"), 8)
    n = 64 * cap
    all_rows = rows[:, 0].reshape(n, d)
    all_grads = rows[:, 1].reshape(n, d)

    part = jnp.stack([dot(w_gate, all_rows, 0, 1), dot(w_up, all_rows, 0, 1), dot(w_down, all_grads, 1, 1)])
    sent = lax.ppermute(
        lax.dynamic_slice_in_dim(part, sent_at, half, axis=1), "c", [(0, 1), (1, 0)]
    )
    part = (lax.dynamic_slice_in_dim(part, kept_at, half, axis=1) + sent).astype(BF16)
    part = part.reshape(3, 4, ff // 8, n).transpose(1, 0, 2, 3)
    gate_sum, up_sum, hidden_grad = total(exchange(part, "zh"))
    sigmoid_gate = jax.nn.sigmoid(gate_sum)
    activated = gate_sum * sigmoid_gate
    own = jnp.stack(
        [
            activated * up_sum,
            hidden_grad * up_sum * sigmoid_gate * (1.0 + gate_sum * (1.0 - sigmoid_gate)),
            hidden_grad * activated,
        ]
    ).astype(BF16)
    full = lax.all_gather(spread(own, "zh", 4), "c", axis=0, tiled=True)
    hidden, d_gate, d_up = (full[:, i].reshape(ff, n) for i in range(3))

    out = dot(hidden, w_down, 0, 0).astype(BF16)
    back = (dot(d_gate, w_gate, 0, 1) + dot(d_up, w_up, 0, 1)).astype(BF16)
    both = jnp.stack([out.reshape(8, 8 * cap, d), back.reshape(8, 8 * cap, d)], axis=1)
    both = lax.optimization_barrier(jnp.sum(exchange(both, ("zl", "x")).astype(F32), axis=0).astype(BF16))
    both = both.reshape(2, 8, cap, d).transpose(1, 0, 2, 3).reshape(8, 2 * cap, d)
    mixed, grad_tokens = place(slots, weights, exchange(both, "y"), tok)

    grad_gate = dot(all_rows, d_gate, 0, 1).astype(BF16)
    grad_up = dot(all_rows, d_up, 0, 1).astype(BF16)
    grad_down = dot(hidden, all_grads, 1, 0).astype(BF16)
    return mixed, grad_tokens, grad_gate[None], grad_up[None], grad_down[None]


def solution(mesh):
    fine = Mesh(mesh.devices.reshape(SIZES), AXES)
    acts = P(DP, TENSOR)
    w_in = P(None, TENSOR, DP)
    w_out = P(None, DP, TENSOR)
    slot = P(DP, None, None)
    return jax.shard_map(
        on_device,
        mesh=fine,
        in_specs=(acts, acts, w_in, w_in, w_out, slot, slot),
        out_specs=(acts, acts, w_in, w_in, w_out),
        check_vma=False,
    )
```

```python
import jax
import jax.numpy as jnp
from jax import lax
from jax.experimental import pallas as pl
from jax.experimental.pallas import tpu as pltpu
from jax.sharding import Mesh
from jax.sharding import PartitionSpec as P

AXES = ("zl", "y", "x", "zh", "c")
SIZES = (2, 8, 4, 4, 2)
DP = ("zl", "y", "x")
TENSOR = ("zh", "c")
BF16 = jnp.bfloat16
F32 = jnp.float32


def exchange(pieces, axes):
    return lax.all_to_all(pieces, axes, split_axis=0, concat_axis=0, tiled=True)


def spread(piece, axes, n):
    return exchange(jnp.broadcast_to(piece[None], (n, *piece.shape)), axes)


def total(pieces):
    out = pieces[0].astype(F32)
    for j in range(1, pieces.shape[0]):
        out = out + pieces[j].astype(F32)
    return out


def dot(a, b, ca, cb):
    return lax.dot_general(a, b, (((ca,), (cb,)), ((), ())), preferred_element_type=F32)


def one_hot(slots_ref, shape, slot_dim, first):
    slot = lax.broadcasted_iota(jnp.int32, shape, slot_dim) - first
    token = lax.broadcasted_iota(jnp.int32, shape, 1 - slot_dim)
    wanted = jnp.full(shape, -1, jnp.int32)
    for s in range(slots_ref.shape[0]):
        wanted = jnp.where(slot == s, slots_ref[s], wanted)
    return (token == wanted).astype(F32).astype(BF16)


def by_slot(weights_ref, rows, first, other):
    slot = lax.broadcasted_iota(jnp.int32, (rows, 1), 0) - first
    out = jnp.full((rows, 1), other, F32)
    for s in range(weights_ref.shape[0]):
        out = jnp.where(slot == s, weights_ref[s], out)
    return out


def pick_body(slots_ref, weights_ref, *refs):
    sources, (out_ref, *weight_refs, tokens_ref, cotangent_ref, sems) = refs[:4], refs[4:]
    copies = [
        pltpu.make_async_copy(src, dst, sems.at[i])
        for i, (src, dst) in enumerate(zip(sources, (tokens_ref, cotangent_ref, *weight_refs)))
    ]
    for copy in copies:
        copy.start()
    cap = slots_ref.shape[0]
    count, rows, _ = out_ref.shape
    hot = one_hot(slots_ref, (rows, tokens_ref.shape[0]), 0, 0)
    hot_d = one_hot(slots_ref, (rows, tokens_ref.shape[0]), 0, cap)
    scale = by_slot(weights_ref, rows, cap, 0.0)
    copies[0].wait()
    copies[1].wait()
    picked = dot(hot, tokens_ref[...], 1, 0)
    packed = (picked + scale * dot(hot_d, cotangent_ref[...], 1, 0)).astype(BF16)
    for j in range(count):
        out_ref[j] = packed
    for copy in copies[2:]:
        copy.wait()


def place_body(hot_ref, scale_ref, pieces_ref, mixed_ref, grad_ref):
    tok = mixed_ref.shape[0]
    acc = pieces_ref[0].astype(F32)
    for j in range(1, pieces_ref.shape[0]):
        acc = acc + pieces_ref[j].astype(F32)
    acc = (acc * scale_ref[:, :1]).astype(BF16)
    mixed_ref[...] = dot(hot_ref[:tok], acc, 1, 0).astype(BF16)
    grad_ref[...] = dot(hot_ref[tok:], acc, 1, 0).astype(BF16)


def regroup_body(pieces_ref, out_ref):
    targets, rows, d = out_ref.shape
    cap = rows // 2
    padded = -(-rows // 8) * 8
    acc = pieces_ref[0].astype(F32)
    for j in range(1, pieces_ref.shape[0]):
        acc = acc + pieces_ref[j].astype(F32)
    acc = acc.reshape(targets * rows, d).astype(BF16)
    shape = (targets * padded, targets * rows)
    at = lax.broadcasted_iota(jnp.int32, shape, 0)
    target, row = at // padded, at % padded
    source = jnp.where(row < cap, target * cap + row, (targets - 1 + target) * cap + row)
    source = jnp.where(row < rows, source, -1)
    move = (lax.broadcasted_iota(jnp.int32, shape, 1) == source).astype(F32).astype(BF16)
    out_ref[...] = dot(move, acc, 1, 0).astype(BF16).reshape(targets, padded, d)[:, :rows]


SMEM = pl.BlockSpec(memory_space=pltpu.SMEM)
VMEM = pl.BlockSpec(memory_space=pltpu.VMEM)
ANY = pl.BlockSpec(memory_space=pl.ANY)


def pick(slots, weights, tokens, cotangent, matrices, copies):
    return pl.pallas_call(
        pick_body,
        in_specs=[SMEM, SMEM, ANY, ANY, ANY, ANY],
        out_specs=(VMEM, VMEM, VMEM),
        out_shape=(
            pltpu.VMEM((copies, 2 * slots.shape[0], tokens.shape[1]), BF16),
            *(pltpu.VMEM(w.shape, BF16) for w in matrices),
        ),
        scratch_shapes=[
            pltpu.VMEM(tokens.shape, BF16),
            pltpu.VMEM(cotangent.shape, BF16),
            pltpu.SemaphoreType.DMA((4,)),
        ],
    )(slots, weights, tokens, cotangent, *matrices)


def on_chip(body, shape, dtype, *arrays):
    return pl.pallas_call(
        body, in_specs=[VMEM] * len(arrays), out_specs=VMEM, out_shape=pltpu.VMEM(shape, dtype)
    )(*(pltpu.with_memory_space_constraint(x, pltpu.VMEM) for x in arrays))


def spots(slots, weights, tok):
    cap = slots.shape[0]
    spot = jnp.concatenate([slots, jnp.where(slots >= 0, slots + tok, -1)])
    hot = (jnp.arange(2 * tok, dtype=jnp.int32)[:, None] == spot[None, :]).astype(BF16)
    scale = jnp.concatenate([weights, jnp.ones((cap,), F32)])
    return hot, jnp.broadcast_to(scale[:, None], (2 * cap, 128))


def place(hot, scale, pieces):
    out = jax.ShapeDtypeStruct((hot.shape[0] // 2, pieces.shape[2]), BF16)
    return pl.pallas_call(place_body, in_specs=[VMEM, VMEM, VMEM], out_specs=(VMEM, VMEM), out_shape=(out, out))(
        *(pltpu.with_memory_space_constraint(x, pltpu.VMEM) for x in (hot, scale, pieces))
    )


def on_device(tokens, cotangent, w_gate, w_up, w_down, slot_token, route_weight):
    w_gate, w_up, w_down = w_gate[0], w_up[0], w_down[0]
    slots, weights = slot_token[0, 0], route_weight[0, 0]
    tok, d = tokens.shape
    cap = slots.shape[0]
    ff = w_gate.shape[1]

    half = ff // 2
    kept_at = lax.axis_index("c").astype(jnp.uint32) * half
    sent_at = half - kept_at
    (near, w_gate, w_up), kept_at, sent_at = lax.optimization_barrier(
        (pick(slots, weights, tokens, cotangent, (w_gate, w_up), 8), kept_at, sent_at)
    )
    near = exchange(near, "y")
    near = near.reshape(8, 2, cap, d).transpose(1, 0, 2, 3).reshape(2, 8 * cap, d)
    rows = spread(near, ("zl", "x"), 8)
    n = 64 * cap

    all_rows, all_grads = (rows[:, i].reshape(n, d) for i in range(2))
    part = jnp.stack([dot(w_gate, all_rows, 0, 1), dot(w_up, all_rows, 0, 1), dot(w_down, all_grads, 1, 1)])
    sent = lax.ppermute(lax.dynamic_slice_in_dim(part, sent_at, half, axis=1), "c", [(0, 1), (1, 0)])
    part = (lax.dynamic_slice_in_dim(part, kept_at, half, axis=1) + sent).astype(BF16)
    part = part.reshape(3, 4, ff // 8, n).transpose(1, 0, 2, 3)
    gate_sum, up_sum, hidden_grad = total(exchange(part, "zh"))
    sigmoid_gate = jax.nn.sigmoid(gate_sum)
    activated = gate_sum * sigmoid_gate
    own = jnp.stack(
        [
            activated * up_sum,
            hidden_grad * up_sum * sigmoid_gate * (1.0 + gate_sum * (1.0 - sigmoid_gate)),
            hidden_grad * activated,
        ]
    ).astype(BF16)
    full = lax.all_gather(spread(own, "zh", 4), "c", axis=0, tiled=True)

    hidden, d_gate, d_up = (full[:, i].reshape(ff, n) for i in range(3))
    out = dot(hidden, w_down, 0, 0).astype(BF16)
    back = (dot(d_gate, w_gate, 0, 1) + dot(d_up, w_up, 0, 1)).astype(BF16)
    both = jnp.stack([out.reshape(8, 8 * cap, d), back.reshape(8, 8 * cap, d)], axis=1)
    both, slots, weights = lax.optimization_barrier((both, slots, weights))
    both = exchange(both, ("zl", "x"))

    grad_gate = dot(all_rows, d_gate, 0, 1).astype(BF16)
    grad_up = dot(all_rows, d_up, 0, 1).astype(BF16)
    grad_down = dot(hidden, all_grads, 1, 0).astype(BF16)
    both, grad_gate, grad_up, grad_down, (hot, scale) = lax.optimization_barrier(
        (both, grad_gate, grad_up, grad_down, spots(slots, weights, tok))
    )
    both = on_chip(regroup_body, (8, 2 * cap, d), BF16, both)
    mixed, grad_tokens = place(hot, scale, exchange(both, "y"))
    return mixed, grad_tokens, grad_gate[None], grad_up[None], grad_down[None]


def solution(mesh):
    fine = Mesh(mesh.devices.reshape(SIZES), AXES)
    acts = P(DP, TENSOR)
    w_in = P(None, TENSOR, DP)
    w_out = P(None, DP, TENSOR)
    slot = P(DP, None, None)
    return jax.shard_map(
        on_device,
        mesh=fine,
        in_specs=(acts, acts, w_in, w_in, w_out, slot, slot),
        out_specs=(acts, acts, w_in, w_in, w_out),
        check_vma=False,
    )
```

```python
import jax
import jax.numpy as jnp
from jax import lax
from jax.experimental import pallas as pl
from jax.experimental.pallas import tpu as pltpu
from jax.sharding import Mesh
from jax.sharding import PartitionSpec as P

AXES = ("zl", "y", "x", "zh", "c")
SIZES = (2, 8, 4, 4, 2)
DP = ("zl", "y", "x")
TENSOR = ("zh", "c")
BF16 = jnp.bfloat16
F32 = jnp.float32


def exchange(pieces, axes):
    return lax.all_to_all(pieces, axes, split_axis=0, concat_axis=0, tiled=True)


def spread(piece, axes, n):
    return exchange(jnp.broadcast_to(piece[None], (n, *piece.shape)), axes)


def total(pieces):
    out = pieces[0].astype(F32)
    for j in range(1, pieces.shape[0]):
        out = out + pieces[j].astype(F32)
    return out


def dot(a, b, ca, cb):
    return lax.dot_general(a, b, (((ca,), (cb,)), ((), ())), preferred_element_type=F32)


def one_hot(slots_ref, shape, slot_dim, first):
    slot = lax.broadcasted_iota(jnp.int32, shape, slot_dim) - first
    token = lax.broadcasted_iota(jnp.int32, shape, 1 - slot_dim)
    wanted = jnp.full(shape, -1, jnp.int32)
    for s in range(slots_ref.shape[0]):
        wanted = jnp.where(slot == s, slots_ref[s], wanted)
    return (token == wanted).astype(F32).astype(BF16)


def by_slot(weights_ref, rows, first, other):
    slot = lax.broadcasted_iota(jnp.int32, (rows, 1), 0) - first
    out = jnp.full((rows, 1), other, F32)
    for s in range(weights_ref.shape[0]):
        out = jnp.where(slot == s, weights_ref[s], out)
    return out


def pick_body(*refs):
    sources, (out_ref, *matrix_refs, slots_ref, weights_ref, tokens_ref, cotangent_ref, sems) = refs[:6], refs[6:]
    targets = (slots_ref, weights_ref, tokens_ref, cotangent_ref, *matrix_refs)
    copies = [pltpu.make_async_copy(src, dst, sems.at[i]) for i, (src, dst) in enumerate(zip(sources, targets))]
    for copy in copies:
        copy.start()
    copies[0].wait()
    copies[1].wait()
    cap = slots_ref.shape[0]
    count, rows, _ = out_ref.shape
    hot = one_hot(slots_ref, (rows, tokens_ref.shape[0]), 0, 0)
    hot_d = one_hot(slots_ref, (rows, tokens_ref.shape[0]), 0, cap)
    scale = by_slot(weights_ref, rows, cap, 0.0)
    copies[2].wait()
    copies[3].wait()
    picked = dot(hot, tokens_ref[...], 1, 0)
    packed = (picked + scale * dot(hot_d, cotangent_ref[...], 1, 0)).astype(BF16)
    for j in range(count):
        out_ref[j] = packed
    for copy in copies[4:]:
        copy.wait()


def place_body(hot_ref, scale_ref, pieces_ref, mixed_ref, grad_ref):
    tok = mixed_ref.shape[0]
    acc = pieces_ref[0].astype(F32)
    for j in range(1, pieces_ref.shape[0]):
        acc = acc + pieces_ref[j].astype(F32)
    acc = (acc * scale_ref[:, :1]).astype(BF16)
    mixed_ref[...] = dot(hot_ref[:tok], acc, 1, 0).astype(BF16)
    grad_ref[...] = dot(hot_ref[tok:], acc, 1, 0).astype(BF16)


def regroup_body(pieces_ref, out_ref):
    targets, rows, d = out_ref.shape
    cap = rows // 2
    padded = -(-rows // 8) * 8
    acc = pieces_ref[0].astype(F32)
    for j in range(1, pieces_ref.shape[0]):
        acc = acc + pieces_ref[j].astype(F32)
    acc = acc.reshape(targets * rows, d).astype(BF16)
    shape = (targets * padded, targets * rows)
    at = lax.broadcasted_iota(jnp.int32, shape, 0)
    target, row = at // padded, at % padded
    source = jnp.where(row < cap, target * cap + row, (targets - 1 + target) * cap + row)
    source = jnp.where(row < rows, source, -1)
    move = (lax.broadcasted_iota(jnp.int32, shape, 1) == source).astype(F32).astype(BF16)
    out_ref[...] = dot(move, acc, 1, 0).astype(BF16).reshape(targets, padded, d)[:, :rows]


VMEM = pl.BlockSpec(memory_space=pltpu.VMEM)
ANY = pl.BlockSpec(memory_space=pl.ANY)


def pick(slots, weights, tokens, cotangent, matrices, copies):
    return pl.pallas_call(
        pick_body,
        in_specs=[ANY] * 6,
        out_specs=(VMEM, VMEM, VMEM),
        out_shape=(
            pltpu.VMEM((copies, 2 * slots.shape[0], tokens.shape[1]), BF16),
            *(pltpu.VMEM(w.shape, BF16) for w in matrices),
        ),
        scratch_shapes=[
            pltpu.SMEM(slots.shape, slots.dtype),
            pltpu.SMEM(weights.shape, weights.dtype),
            pltpu.VMEM(tokens.shape, BF16),
            pltpu.VMEM(cotangent.shape, BF16),
            pltpu.SemaphoreType.DMA((6,)),
        ],
    )(slots, weights, tokens, cotangent, *matrices)


def on_chip(body, shape, dtype, *arrays):
    return pl.pallas_call(
        body, in_specs=[VMEM] * len(arrays), out_specs=VMEM, out_shape=pltpu.VMEM(shape, dtype)
    )(*(pltpu.with_memory_space_constraint(x, pltpu.VMEM) for x in arrays))


def spots(slots, weights, tok):
    cap = slots.shape[0]
    spot = jnp.concatenate([slots, jnp.where(slots >= 0, slots + tok, -1)])
    hot = (jnp.arange(2 * tok, dtype=jnp.int32)[:, None] == spot[None, :]).astype(BF16)
    scale = jnp.concatenate([weights, jnp.ones((cap,), F32)])
    return hot, jnp.broadcast_to(scale[:, None], (2 * cap, 128))


def place(hot, scale, pieces):
    out = jax.ShapeDtypeStruct((hot.shape[0] // 2, pieces.shape[2]), BF16)
    return pl.pallas_call(place_body, in_specs=[VMEM, VMEM, VMEM], out_specs=(VMEM, VMEM), out_shape=(out, out))(
        *(pltpu.with_memory_space_constraint(x, pltpu.VMEM) for x in (hot, scale, pieces))
    )


def on_device(tokens, cotangent, w_gate, w_up, w_down, slot_token, route_weight):
    w_gate, w_up, w_down = w_gate[0], w_up[0], w_down[0]
    slots, weights = slot_token[0, 0], route_weight[0, 0]
    tok, d = tokens.shape
    cap = slots.shape[0]
    ff = w_gate.shape[1]

    half = ff // 2
    other = 1 - lax.axis_index("c").astype(jnp.uint32)
    sent_at = other * half
    kept_at = half - sent_at
    (near, w_gate, w_up), other, kept_at, sent_at = lax.optimization_barrier(
        (pick(slots, weights, tokens, cotangent, (w_gate, w_up), 8), other, kept_at, sent_at)
    )
    near = exchange(near, "y")
    near = near.reshape(8, 2, cap, d).transpose(1, 0, 2, 3).reshape(2, 8 * cap, d)
    rows = spread(near, ("zl", "x"), 8)
    n = 64 * cap

    all_rows, all_grads = (rows[:, i].reshape(n, d) for i in range(2))
    part = jnp.stack([dot(w_gate, all_rows, 0, 1), dot(w_up, all_rows, 0, 1), dot(w_down, all_grads, 1, 1)])
    sent = lax.all_gather(lax.dynamic_slice_in_dim(part, sent_at, half, axis=1).astype(BF16), "c")
    sent = lax.dynamic_index_in_dim(sent, other, axis=0, keepdims=False)
    part = (lax.dynamic_slice_in_dim(part, kept_at, half, axis=1) + sent.astype(F32)).astype(BF16)
    part = part.reshape(3, 4, ff // 8, n).transpose(1, 0, 2, 3)
    gate_sum, up_sum, hidden_grad = total(exchange(part, "zh"))
    sigmoid_gate = jax.nn.sigmoid(gate_sum)
    activated = gate_sum * sigmoid_gate
    own = jnp.stack(
        [
            activated * up_sum,
            hidden_grad * up_sum * sigmoid_gate * (1.0 + gate_sum * (1.0 - sigmoid_gate)),
            hidden_grad * activated,
        ]
    ).astype(BF16)
    full = lax.all_gather(spread(own, "zh", 4), "c", axis=0, tiled=True)

    hidden, d_gate, d_up = (full[:, i].reshape(ff, n) for i in range(3))
    out = dot(hidden, w_down, 0, 0).astype(BF16)
    back = (dot(d_gate, w_gate, 0, 1) + dot(d_up, w_up, 0, 1)).astype(BF16)
    both = jnp.stack([out.reshape(8, 8 * cap, d), back.reshape(8, 8 * cap, d)], axis=1)
    both, slots, weights = lax.optimization_barrier((both, slots, weights))
    both = exchange(both, ("zl", "x"))

    grad_gate = dot(all_rows, d_gate, 0, 1).astype(BF16)
    grad_up = dot(all_rows, d_up, 0, 1).astype(BF16)
    grad_down = dot(hidden, all_grads, 1, 0).astype(BF16)
    both, grad_gate, grad_up, grad_down, (hot, scale) = lax.optimization_barrier(
        (both, grad_gate, grad_up, grad_down, spots(slots, weights, tok))
    )
    both = on_chip(regroup_body, (8, 2 * cap, d), BF16, both)
    mixed, grad_tokens = place(hot, scale, exchange(both, "y"))
    return mixed, grad_tokens, grad_gate[None], grad_up[None], grad_down[None]


def solution(mesh):
    fine = Mesh(mesh.devices.reshape(SIZES), AXES)
    acts = P(DP, TENSOR)
    w_in = P(None, TENSOR, DP)
    w_out = P(None, DP, TENSOR)
    slot = P(DP, None, None)
    return jax.shard_map(
        on_device,
        mesh=fine,
        in_specs=(acts, acts, w_in, w_in, w_out, slot, slot),
        out_specs=(acts, acts, w_in, w_in, w_out),
        check_vma=False,
    )
```

```python
import jax
import jax.numpy as jnp
from jax import lax
from jax.experimental import pallas as pl
from jax.experimental.pallas import tpu as pltpu
from jax.sharding import Mesh
from jax.sharding import PartitionSpec as P

AXES = ("zl", "y", "x", "zh", "c")
SIZES = (2, 8, 4, 4, 2)
DP = ("zl", "y", "x")
TENSOR = ("zh", "c")
BF16 = jnp.bfloat16
F32 = jnp.float32


def exchange(pieces, axes):
    return lax.all_to_all(pieces, axes, split_axis=0, concat_axis=0, tiled=True)


def spread(piece, axes, n):
    return exchange(jnp.broadcast_to(piece[None], (n, *piece.shape)), axes)


def total(pieces):
    out = pieces[0].astype(F32)
    for j in range(1, pieces.shape[0]):
        out = out + pieces[j].astype(F32)
    return out


def dot(a, b, ca, cb):
    return lax.dot_general(a, b, (((ca,), (cb,)), ((), ())), preferred_element_type=F32)


def one_hot(slots_ref, shape, slot_dim, first):
    slot = lax.broadcasted_iota(jnp.int32, shape, slot_dim) - first
    token = lax.broadcasted_iota(jnp.int32, shape, 1 - slot_dim)
    wanted = jnp.full(shape, -1, jnp.int32)
    for s in range(slots_ref.shape[0]):
        wanted = jnp.where(slot == s, slots_ref[s], wanted)
    return (token == wanted).astype(F32).astype(BF16)


def by_slot(weights_ref, rows, first, other):
    slot = lax.broadcasted_iota(jnp.int32, (rows, 1), 0) - first
    out = jnp.full((rows, 1), other, F32)
    for s in range(weights_ref.shape[0]):
        out = jnp.where(slot == s, weights_ref[s], out)
    return out


def pick_body(*refs):
    sources, (out_ref, *matrix_refs, slots_ref, weights_ref, tokens_ref, cotangent_ref, sems) = refs[:6], refs[6:]
    targets = (slots_ref, weights_ref, tokens_ref, cotangent_ref, *matrix_refs)
    copies = [pltpu.make_async_copy(src, dst, sems.at[i]) for i, (src, dst) in enumerate(zip(sources, targets))]
    for copy in copies:
        copy.start()
    copies[0].wait()
    copies[1].wait()
    cap = slots_ref.shape[0]
    count, rows, half = out_ref.shape
    hots = [one_hot(slots_ref, (rows, tokens_ref.shape[0]), 0, k * cap) for k in range(4)]
    scale = by_slot(weights_ref, rows, cap, 0.0) + by_slot(weights_ref, rows, 3 * cap, 0.0)
    copies[2].wait()
    copies[3].wait()
    picked = dot(hots[0], tokens_ref[:, :half], 1, 0) + dot(hots[2], tokens_ref[:, half:], 1, 0)
    d_rows = dot(hots[1], cotangent_ref[:, :half], 1, 0) + dot(hots[3], cotangent_ref[:, half:], 1, 0)
    packed = (picked + scale * d_rows).astype(BF16)
    for j in range(count):
        out_ref[j] = packed
    for copy in copies[4:]:
        copy.wait()


def place_body(hot_ref, scale_ref, pieces_ref, mixed_ref, grad_ref):
    tok = mixed_ref.shape[0]
    half = pieces_ref.shape[2]
    acc = pieces_ref[0].astype(F32)
    for j in range(1, pieces_ref.shape[0]):
        acc = acc + pieces_ref[j].astype(F32)
    acc = (acc * scale_ref[:, :1]).astype(BF16)
    for p in range(2):
        cols = slice(p * half, (p + 1) * half)
        mixed_ref[:, cols] = dot(hot_ref[2 * p * tok : (2 * p + 1) * tok], acc, 1, 0).astype(BF16)
        grad_ref[:, cols] = dot(hot_ref[(2 * p + 1) * tok : (2 * p + 2) * tok], acc, 1, 0).astype(BF16)


def moves(blocks, cap, p):
    shape = (2 * blocks * cap, 4 * blocks * cap)
    row = lax.broadcasted_iota(jnp.int32, (shape[0], 1), 0)
    kind = (row >= blocks * cap).astype(jnp.int32)
    block = sum((row - kind * blocks * cap >= b * cap).astype(jnp.int32) for b in range(1, blocks))
    at = row + block * 3 * cap + 2 * p * cap + kind * (cap - blocks * cap)
    return (lax.broadcasted_iota(jnp.int32, shape, 1) == at).astype(F32).astype(BF16)


def near_body(pieces_ref, out_ref):
    blocks, rows, half = pieces_ref.shape
    count, _, kept, d = out_ref.shape
    pieces = pieces_ref[...].reshape(blocks * rows, half)
    both = [dot(moves(blocks, rows // 4, p), pieces, 1, 0).astype(BF16) for p in range(2)]
    both = jnp.concatenate(both, axis=1).reshape(2, kept, d)
    for j in range(count):
        out_ref[j] = both


def regroup_body(pieces_ref, out_ref):
    blocks, rows, half = out_ref.shape
    acc = pieces_ref[0].astype(F32)
    for j in range(1, pieces_ref.shape[0]):
        acc = acc + pieces_ref[j].astype(F32)
    acc = acc.reshape(-1, 2 * half).astype(BF16)
    out = sum(dot(moves(blocks, rows // 4, p), acc[:, p * half : (p + 1) * half], 0, 0) for p in range(2))
    out_ref[...] = out.astype(BF16).reshape(out_ref.shape)


VMEM = pl.BlockSpec(memory_space=pltpu.VMEM)
ANY = pl.BlockSpec(memory_space=pl.ANY)


def pick(slots, weights, tokens, cotangent, matrices, copies):
    return pl.pallas_call(
        pick_body,
        in_specs=[ANY] * 6,
        out_specs=(VMEM, VMEM, VMEM),
        out_shape=(
            pltpu.VMEM((copies, 4 * slots.shape[0], tokens.shape[1] // 2), BF16),
            *(pltpu.VMEM(w.shape, BF16) for w in matrices),
        ),
        scratch_shapes=[
            pltpu.SMEM(slots.shape, slots.dtype),
            pltpu.SMEM(weights.shape, weights.dtype),
            pltpu.VMEM(tokens.shape, BF16),
            pltpu.VMEM(cotangent.shape, BF16),
            pltpu.SemaphoreType.DMA((6,)),
        ],
    )(slots, weights, tokens, cotangent, *matrices)


def on_chip(body, shape, dtype, *arrays):
    return pl.pallas_call(
        body, in_specs=[VMEM] * len(arrays), out_specs=VMEM, out_shape=pltpu.VMEM(shape, dtype)
    )(*(pltpu.with_memory_space_constraint(x, pltpu.VMEM) for x in arrays))


def spots(slots, weights, tok):
    used = slots >= 0
    spot = jnp.concatenate([jnp.where(used, slots + k * tok, -1) for k in range(4)])
    hot = (jnp.arange(4 * tok, dtype=jnp.int32)[:, None] == spot[None, :]).astype(BF16)
    scale = jnp.concatenate([weights, jnp.ones_like(weights), weights, jnp.ones_like(weights)])
    return hot, jnp.broadcast_to(scale[:, None], (scale.shape[0], 128))


def place(hot, scale, pieces):
    out = jax.ShapeDtypeStruct((hot.shape[0] // 4, 2 * pieces.shape[2]), BF16)
    return pl.pallas_call(place_body, in_specs=[VMEM, VMEM, VMEM], out_specs=(VMEM, VMEM), out_shape=(out, out))(
        *(pltpu.with_memory_space_constraint(x, pltpu.VMEM) for x in (hot, scale, pieces))
    )


def on_device(tokens, cotangent, w_gate, w_up, w_down, slot_token, route_weight):
    w_gate, w_up, w_down = w_gate[0], w_up[0], w_down[0]
    slots, weights = slot_token[0, 0], route_weight[0, 0]
    tok, d = tokens.shape
    cap = slots.shape[0]
    ff = w_gate.shape[1]

    half = ff // 2
    other = 1 - lax.axis_index("c").astype(jnp.uint32)
    sent_at = other * half
    kept_at = half - sent_at
    (near, w_gate, w_up), other, kept_at, sent_at = lax.optimization_barrier(
        (pick(slots, weights, tokens, cotangent, (w_gate, w_up), 8), other, kept_at, sent_at)
    )
    rows = exchange(on_chip(near_body, (8, 2, 8 * cap, d), BF16, exchange(near, "y")), ("zl", "x"))
    n = 64 * cap

    all_rows, all_grads = (rows[:, i].reshape(n, d) for i in range(2))
    part = jnp.stack([dot(w_gate, all_rows, 0, 1), dot(w_up, all_rows, 0, 1), dot(w_down, all_grads, 1, 1)])
    sent = lax.all_gather(lax.dynamic_slice_in_dim(part, sent_at, half, axis=1).astype(BF16), "c")
    sent = lax.dynamic_index_in_dim(sent, other, axis=0, keepdims=False)
    part = (lax.dynamic_slice_in_dim(part, kept_at, half, axis=1) + sent.astype(F32)).astype(BF16)
    part = part.reshape(3, 4, ff // 8, n).transpose(1, 0, 2, 3)
    gate_sum, up_sum, hidden_grad = total(exchange(part, "zh"))
    sigmoid_gate = jax.nn.sigmoid(gate_sum)
    activated = gate_sum * sigmoid_gate
    own = jnp.stack(
        [
            activated * up_sum,
            hidden_grad * up_sum * sigmoid_gate * (1.0 + gate_sum * (1.0 - sigmoid_gate)),
            hidden_grad * activated,
        ]
    ).astype(BF16)
    full = lax.all_gather(spread(own, "zh", 4), "c", axis=0, tiled=True)

    hidden, d_gate, d_up = (full[:, i].reshape(ff, n) for i in range(3))
    out = dot(hidden, w_down, 0, 0).astype(BF16)
    back = (dot(d_gate, w_gate, 0, 1) + dot(d_up, w_up, 0, 1)).astype(BF16)
    both = jnp.stack([out.reshape(8, 8 * cap, d), back.reshape(8, 8 * cap, d)], axis=1)
    both, slots, weights = lax.optimization_barrier((both, slots, weights))
    both = exchange(both, ("zl", "x"))

    grad_gate = dot(all_rows, d_gate, 0, 1).astype(BF16)
    grad_up = dot(all_rows, d_up, 0, 1).astype(BF16)
    grad_down = dot(hidden, all_grads, 1, 0).astype(BF16)
    both, grad_gate, grad_up, grad_down, (hot, scale) = lax.optimization_barrier(
        (both, grad_gate, grad_up, grad_down, spots(slots, weights, tok))
    )
    both = on_chip(regroup_body, (8, 4 * cap, d // 2), BF16, both)
    mixed, grad_tokens = place(hot, scale, exchange(both, "y"))
    return mixed, grad_tokens, grad_gate[None], grad_up[None], grad_down[None]


def solution(mesh):
    fine = Mesh(mesh.devices.reshape(SIZES), AXES)
    acts = P(DP, TENSOR)
    w_in = P(None, TENSOR, DP)
    w_out = P(None, DP, TENSOR)
    slot = P(DP, None, None)
    return jax.shard_map(
        on_device,
        mesh=fine,
        in_specs=(acts, acts, w_in, w_in, w_out, slot, slot),
        out_specs=(acts, acts, w_in, w_in, w_out),
        check_vma=False,
    )
```

```python
import jax
import jax.numpy as jnp
from jax import lax
from jax.experimental import pallas as pl
from jax.experimental.pallas import tpu as pltpu
from jax.sharding import Mesh
from jax.sharding import PartitionSpec as P

AXES = ("zl", "y", "x", "zh", "c")
SIZES = (2, 8, 4, 4, 2)
DP = ("zl", "y", "x")
TENSOR = ("zh", "c")
BF16 = jnp.bfloat16
F32 = jnp.float32


def exchange(pieces, axes):
    return lax.all_to_all(pieces, axes, split_axis=0, concat_axis=0, tiled=True)


def spread(piece, axes, n):
    return exchange(jnp.broadcast_to(piece[None], (n, *piece.shape)), axes)


def total(pieces):
    out = pieces[0].astype(F32)
    for j in range(1, pieces.shape[0]):
        out = out + pieces[j].astype(F32)
    return out


def dot(a, b, ca, cb):
    return lax.dot_general(a, b, (((ca,), (cb,)), ((), ())), preferred_element_type=F32)


def one_hot(slots_ref, shape, slot_dim, first):
    slot = lax.broadcasted_iota(jnp.int32, shape, slot_dim) - first
    token = lax.broadcasted_iota(jnp.int32, shape, 1 - slot_dim)
    wanted = jnp.full(shape, -1, jnp.int32)
    for s in range(slots_ref.shape[0]):
        wanted = jnp.where(slot == s, slots_ref[s], wanted)
    return (token == wanted).astype(F32).astype(BF16)


def by_slot(weights_ref, rows, first, other):
    slot = lax.broadcasted_iota(jnp.int32, (rows, 1), 0) - first
    out = jnp.full((rows, 1), other, F32)
    for s in range(weights_ref.shape[0]):
        out = jnp.where(slot == s, weights_ref[s], out)
    return out


def pick_body(*refs):
    sources, (out_ref, *matrix_refs, slots_ref, weights_ref, tokens_ref, cotangent_ref, sems) = refs[:6], refs[6:]
    targets = (slots_ref, weights_ref, tokens_ref, cotangent_ref, *matrix_refs)
    copies = [pltpu.make_async_copy(src, dst, sems.at[i]) for i, (src, dst) in enumerate(zip(sources, targets))]
    for copy in copies:
        copy.start()
    copies[0].wait()
    copies[1].wait()
    cap = slots_ref.shape[0]
    count, rows, half = out_ref.shape
    hots = [one_hot(slots_ref, (rows, tokens_ref.shape[0]), 0, k * cap) for k in range(4)]
    scale = by_slot(weights_ref, rows, cap, 0.0) + by_slot(weights_ref, rows, 3 * cap, 0.0)
    copies[2].wait()
    copies[3].wait()
    picked = dot(hots[0], tokens_ref[:, :half], 1, 0) + dot(hots[2], tokens_ref[:, half:], 1, 0)
    d_rows = dot(hots[1], cotangent_ref[:, :half], 1, 0) + dot(hots[3], cotangent_ref[:, half:], 1, 0)
    packed = (picked + scale * d_rows).astype(BF16)
    for j in range(count):
        out_ref[j] = packed
    for copy in copies[4:]:
        copy.wait()


def place_body(hot_ref, scale_ref, pieces_ref, *refs):
    half = pieces_ref.shape[2]
    tok = hot_ref.shape[0] // 4
    acc = pieces_ref[0].astype(F32)
    for j in range(1, pieces_ref.shape[0]):
        acc = acc + pieces_ref[j].astype(F32)
    acc = (acc * scale_ref[:, :1]).astype(BF16)
    sems = refs[4]
    copies = [pltpu.make_async_copy(refs[2 + k], refs[k], sems.at[k]) for k in range(2)]
    for k in range(2):
        for p in range(2):
            hot = hot_ref[(2 * p + k) * tok : (2 * p + k + 1) * tok]
            refs[2 + k][:, p * half : (p + 1) * half] = dot(hot, acc, 1, 0).astype(BF16)
        copies[k].start()
    for copy in copies:
        copy.wait()


def moves(blocks, cap, p):
    shape = (2 * blocks * cap, 4 * blocks * cap)
    row = lax.broadcasted_iota(jnp.int32, (shape[0], 1), 0)
    kind = (row >= blocks * cap).astype(jnp.int32)
    block = sum((row - kind * blocks * cap >= b * cap).astype(jnp.int32) for b in range(1, blocks))
    at = row + block * 3 * cap + 2 * p * cap + kind * (cap - blocks * cap)
    return (lax.broadcasted_iota(jnp.int32, shape, 1) == at).astype(F32).astype(BF16)


def near_body(pieces_ref, out_ref):
    blocks, rows, half = pieces_ref.shape
    count, _, kept, d = out_ref.shape
    pieces = pieces_ref[...].reshape(blocks * rows, half)
    both = [dot(moves(blocks, rows // 4, p), pieces, 1, 0).astype(BF16) for p in range(2)]
    both = jnp.concatenate(both, axis=1).reshape(2, kept, d)
    for j in range(count):
        out_ref[j] = both


def slot_body(out_ref, full_ref, w_gate_ref, w_up_ref, both_ref, back_ref, sems):
    first = pltpu.make_async_copy(out_ref, both_ref.at[:, 0], sems.at[0])
    first.start()
    n = full_ref.shape[3]
    d_gate, d_up = (full_ref[:, i].reshape(-1, n).T for i in (1, 2))
    back = dot(d_gate, w_gate_ref[...], 1, 1) + dot(d_up, w_up_ref[...], 1, 1)
    back_ref[...] = back.astype(BF16).reshape(back_ref.shape)
    second = pltpu.make_async_copy(back_ref, both_ref.at[:, 1], sems.at[1])
    second.start()
    first.wait()
    second.wait()


def regroup_body(pieces_ref, out_ref):
    blocks, rows, half = out_ref.shape
    acc = pieces_ref[0].astype(F32)
    for j in range(1, pieces_ref.shape[0]):
        acc = acc + pieces_ref[j].astype(F32)
    acc = acc.reshape(-1, 2 * half).astype(BF16)
    out = sum(dot(moves(blocks, rows // 4, p), acc[:, p * half : (p + 1) * half], 0, 0) for p in range(2))
    out_ref[...] = out.astype(BF16).reshape(out_ref.shape)


VMEM = pl.BlockSpec(memory_space=pltpu.VMEM)
ANY = pl.BlockSpec(memory_space=pl.ANY)


def pick(slots, weights, tokens, cotangent, matrices, copies):
    return pl.pallas_call(
        pick_body,
        in_specs=[ANY] * 6,
        out_specs=(VMEM, VMEM, VMEM),
        out_shape=(
            pltpu.VMEM((copies, 4 * slots.shape[0], tokens.shape[1] // 2), BF16),
            *(pltpu.VMEM(w.shape, BF16) for w in matrices),
        ),
        scratch_shapes=[
            pltpu.SMEM(slots.shape, slots.dtype),
            pltpu.SMEM(weights.shape, weights.dtype),
            pltpu.VMEM(tokens.shape, BF16),
            pltpu.VMEM(cotangent.shape, BF16),
            pltpu.SemaphoreType.DMA((6,)),
        ],
    )(slots, weights, tokens, cotangent, *matrices)


def on_chip(body, shape, dtype, *arrays):
    return pl.pallas_call(
        body, in_specs=[VMEM] * len(arrays), out_specs=VMEM, out_shape=pltpu.VMEM(shape, dtype)
    )(*(pltpu.with_memory_space_constraint(x, pltpu.VMEM) for x in arrays))


def pair(out, full, w_gate, w_up):
    groups, rows, d = out.shape
    return pl.pallas_call(
        slot_body,
        in_specs=[VMEM] * 4,
        out_specs=ANY,
        out_shape=jax.ShapeDtypeStruct((groups, 2, rows, d), BF16),
        scratch_shapes=[pltpu.VMEM(out.shape, BF16), pltpu.SemaphoreType.DMA((2,))],
    )(*(pltpu.with_memory_space_constraint(x, pltpu.VMEM) for x in (out, full, w_gate, w_up)))


def spots(slots, weights, tok):
    used = slots >= 0
    spot = jnp.concatenate([jnp.where(used, slots + k * tok, -1) for k in range(4)])
    hot = (jnp.arange(4 * tok, dtype=jnp.int32)[:, None] == spot[None, :]).astype(BF16)
    scale = jnp.concatenate([weights, jnp.ones_like(weights), weights, jnp.ones_like(weights)])
    return hot, jnp.broadcast_to(scale[:, None], (scale.shape[0], 128))


def place(hot, scale, pieces):
    out = jax.ShapeDtypeStruct((hot.shape[0] // 4, 2 * pieces.shape[2]), BF16)
    return pl.pallas_call(
        place_body,
        in_specs=[VMEM] * 3,
        out_specs=(ANY, ANY),
        out_shape=(out, out),
        scratch_shapes=[pltpu.VMEM(out.shape, BF16), pltpu.VMEM(out.shape, BF16), pltpu.SemaphoreType.DMA((2,))],
    )(*(pltpu.with_memory_space_constraint(x, pltpu.VMEM) for x in (hot, scale, pieces)))


def on_device(tokens, cotangent, w_gate, w_up, w_down, slot_token, route_weight):
    w_gate, w_up, w_down = w_gate[0], w_up[0], w_down[0]
    slots, weights = slot_token[0, 0], route_weight[0, 0]
    tok, d = tokens.shape
    cap = slots.shape[0]
    ff = w_gate.shape[1]

    half = ff // 2
    other = 1 - lax.axis_index("c").astype(jnp.uint32)
    sent_at = other * half
    kept_at = half - sent_at
    (near, w_gate, w_up), other, kept_at, sent_at = lax.optimization_barrier(
        (pick(slots, weights, tokens, cotangent, (w_gate, w_up), 8), other, kept_at, sent_at)
    )
    rows = exchange(on_chip(near_body, (8, 2, 8 * cap, d), BF16, exchange(near, "y")), ("zl", "x"))
    n = 64 * cap

    all_rows, all_grads = (rows[:, i].reshape(n, d) for i in range(2))
    part = jnp.stack([dot(w_gate, all_rows, 0, 1), dot(w_up, all_rows, 0, 1), dot(w_down, all_grads, 1, 1)])
    sent = lax.all_gather(lax.dynamic_slice_in_dim(part, sent_at, half, axis=1).astype(BF16), "c")
    sent = lax.dynamic_index_in_dim(sent, other, axis=0, keepdims=False)
    part = (lax.dynamic_slice_in_dim(part, kept_at, half, axis=1) + sent.astype(F32)).astype(BF16)
    part = part.reshape(3, 4, ff // 8, n).transpose(1, 0, 2, 3)
    gate_sum, up_sum, hidden_grad = total(exchange(part, "zh"))
    sigmoid_gate = jax.nn.sigmoid(gate_sum)
    activated = gate_sum * sigmoid_gate
    own = jnp.stack(
        [
            activated * up_sum,
            hidden_grad * up_sum * sigmoid_gate * (1.0 + gate_sum * (1.0 - sigmoid_gate)),
            hidden_grad * activated,
        ]
    ).astype(BF16)
    full = lax.all_gather(spread(own, "zh", 4), "c", axis=0, tiled=True)

    hidden, d_gate, d_up = (full[:, i].reshape(ff, n) for i in range(3))
    out = dot(hidden, w_down, 0, 0).astype(BF16)
    both = pair(out.reshape(8, 8 * cap, d), full, w_gate, w_up)
    both, slots, weights = lax.optimization_barrier((both, slots, weights))
    both = exchange(both, ("zl", "x"))

    grad_gate = dot(all_rows, d_gate, 0, 1).astype(BF16)
    grad_up = dot(all_rows, d_up, 0, 1).astype(BF16)
    grad_down = dot(hidden, all_grads, 1, 0).astype(BF16)
    both, grad_gate, grad_up, grad_down, (hot, scale) = lax.optimization_barrier(
        (both, grad_gate, grad_up, grad_down, spots(slots, weights, tok))
    )
    both = on_chip(regroup_body, (8, 4 * cap, d // 2), BF16, both)
    mixed, grad_tokens = place(hot, scale, exchange(both, "y"))
    return mixed, grad_tokens, grad_gate[None], grad_up[None], grad_down[None]


def solution(mesh):
    fine = Mesh(mesh.devices.reshape(SIZES), AXES)
    acts = P(DP, TENSOR)
    w_in = P(None, TENSOR, DP)
    w_out = P(None, DP, TENSOR)
    slot = P(DP, None, None)
    return jax.shard_map(
        on_device,
        mesh=fine,
        in_specs=(acts, acts, w_in, w_in, w_out, slot, slot),
        out_specs=(acts, acts, w_in, w_in, w_out),
        check_vma=False,
    )
```

```python
import jax
import jax.numpy as jnp
from jax import lax
from jax.experimental import pallas as pl
from jax.experimental.pallas import tpu as pltpu
from jax.sharding import Mesh
from jax.sharding import PartitionSpec as P

AXES = ("zl", "y", "x", "zh", "c")
SIZES = (2, 8, 4, 4, 2)
DP = ("zl", "y", "x")
TENSOR = ("zh", "c")
BF16 = jnp.bfloat16
F32 = jnp.float32


def exchange(pieces, axes):
    return lax.all_to_all(pieces, axes, split_axis=0, concat_axis=0, tiled=True)


def spread(piece, axes, n):
    return exchange(jnp.broadcast_to(piece[None], (n, *piece.shape)), axes)


def total(pieces):
    out = pieces[0].astype(F32)
    for j in range(1, pieces.shape[0]):
        out = out + pieces[j].astype(F32)
    return out


def dot(a, b, ca, cb):
    return lax.dot_general(a, b, (((ca,), (cb,)), ((), ())), preferred_element_type=F32)


def one_hot(slots_ref, shape, slot_dim, first):
    slot = lax.broadcasted_iota(jnp.int32, shape, slot_dim) - first
    token = lax.broadcasted_iota(jnp.int32, shape, 1 - slot_dim)
    wanted = jnp.full(shape, -1, jnp.int32)
    for s in range(slots_ref.shape[0]):
        wanted = jnp.where(slot == s, slots_ref[s], wanted)
    return (token == wanted).astype(F32).astype(BF16)


def by_slot(weights_ref, rows, first, other):
    slot = lax.broadcasted_iota(jnp.int32, (rows, 1), 0) - first
    out = jnp.full((rows, 1), other, F32)
    for s in range(weights_ref.shape[0]):
        out = jnp.where(slot == s, weights_ref[s], out)
    return out


def pick_body(*refs):
    sources, (out_ref, *matrix_refs, slots_ref, weights_ref, tokens_ref, cotangent_ref, sems) = refs[:6], refs[6:]
    targets = (slots_ref, weights_ref, tokens_ref, cotangent_ref, *matrix_refs)
    copies = [pltpu.make_async_copy(src, dst, sems.at[i]) for i, (src, dst) in enumerate(zip(sources, targets))]
    for copy in copies:
        copy.start()
    copies[0].wait()
    copies[1].wait()
    cap = slots_ref.shape[0]
    count, rows, half = out_ref.shape
    hots = [one_hot(slots_ref, (rows, tokens_ref.shape[0]), 0, k * cap) for k in range(4)]
    scale = by_slot(weights_ref, rows, cap, 0.0) + by_slot(weights_ref, rows, 3 * cap, 0.0)
    copies[2].wait()
    copies[3].wait()
    picked = dot(hots[0], tokens_ref[:, :half], 1, 0) + dot(hots[2], tokens_ref[:, half:], 1, 0)
    d_rows = dot(hots[1], cotangent_ref[:, :half], 1, 0) + dot(hots[3], cotangent_ref[:, half:], 1, 0)
    packed = (picked + scale * d_rows).astype(BF16)
    for j in range(count):
        out_ref[j] = packed
    for copy in copies[4:]:
        copy.wait()


def place_body(hot_ref, scale_ref, pieces_ref, *refs):
    half = pieces_ref.shape[2]
    tok = hot_ref.shape[0] // 4
    acc = pieces_ref[0].astype(F32)
    for j in range(1, pieces_ref.shape[0]):
        acc = acc + pieces_ref[j].astype(F32)
    acc = (acc * scale_ref[:, :1]).astype(BF16)
    sems = refs[4]
    copies = [pltpu.make_async_copy(refs[2 + k], refs[k], sems.at[k]) for k in range(2)]
    for k in range(2):
        for p in range(2):
            hot = hot_ref[(2 * p + k) * tok : (2 * p + k + 1) * tok]
            refs[2 + k][:, p * half : (p + 1) * half] = dot(hot, acc, 1, 0).astype(BF16)
        copies[k].start()
    for copy in copies:
        copy.wait()


def moves(blocks, cap, p):
    shape = (2 * blocks * cap, 4 * blocks * cap)
    row = lax.broadcasted_iota(jnp.int32, (shape[0], 1), 0)
    kind = (row >= blocks * cap).astype(jnp.int32)
    block = sum((row - kind * blocks * cap >= b * cap).astype(jnp.int32) for b in range(1, blocks))
    at = row + block * 3 * cap + 2 * p * cap + kind * (cap - blocks * cap)
    return (lax.broadcasted_iota(jnp.int32, shape, 1) == at).astype(F32).astype(BF16)


def near_body(pieces_ref, out_ref):
    blocks, rows, half = pieces_ref.shape
    count, _, kept, d = out_ref.shape
    pieces = pieces_ref[...].reshape(blocks * rows, half)
    both = [dot(moves(blocks, rows // 4, p), pieces, 1, 0).astype(BF16) for p in range(2)]
    both = jnp.concatenate(both, axis=1).reshape(2, kept, d)
    for j in range(count):
        out_ref[j] = both


def slot_body(out_ref, full_ref, w_gate_ref, w_up_ref, both_ref, back_ref, sems):
    copies = [pltpu.make_async_copy(out_ref, both_ref.at[:, 0], sems.at[0])]
    copies[0].start()
    groups, rows, d = out_ref.shape
    n = full_ref.shape[3]
    d_gate, d_up = (full_ref[:, i].reshape(-1, n).T for i in (1, 2))
    part = groups // 2
    for j in range(2):
        here = pl.ds(j * part, part)
        take = slice(j * part * rows, (j + 1) * part * rows)
        back = dot(d_gate[take], w_gate_ref[...], 1, 1) + dot(d_up[take], w_up_ref[...], 1, 1)
        back_ref[here] = back.astype(BF16).reshape(part, rows, d)
        copies.append(pltpu.make_async_copy(back_ref.at[here], both_ref.at[here, 1], sems.at[1 + j]))
        copies[-1].start()
    for copy in copies:
        copy.wait()


def spot_body(slots_ref, weights_ref, hot_ref, scale_ref):
    cap = slots_ref.shape[0]
    tok = hot_ref.shape[0] // 4
    for k in range(4):
        hot_ref[k * tok : (k + 1) * tok] = one_hot(slots_ref, (tok, 4 * cap), 1, k * cap)
    slot = lax.broadcasted_iota(jnp.int32, scale_ref.shape, 0)
    scale = jnp.ones(scale_ref.shape, F32)
    for s in range(cap):
        scale = jnp.where((slot == s) | (slot == 2 * cap + s), weights_ref[s], scale)
    scale_ref[...] = scale


def regroup_body(pieces_ref, out_ref):
    blocks, rows, half = out_ref.shape
    acc = pieces_ref[0].astype(F32)
    for j in range(1, pieces_ref.shape[0]):
        acc = acc + pieces_ref[j].astype(F32)
    acc = acc.reshape(-1, 2 * half).astype(BF16)
    out = sum(dot(moves(blocks, rows // 4, p), acc[:, p * half : (p + 1) * half], 0, 0) for p in range(2))
    out_ref[...] = out.astype(BF16).reshape(out_ref.shape)


SMEM = pl.BlockSpec(memory_space=pltpu.SMEM)
VMEM = pl.BlockSpec(memory_space=pltpu.VMEM)
ANY = pl.BlockSpec(memory_space=pl.ANY)


def pick(slots, weights, tokens, cotangent, matrices, copies):
    return pl.pallas_call(
        pick_body,
        in_specs=[ANY] * 6,
        out_specs=(VMEM, VMEM, VMEM),
        out_shape=(
            pltpu.VMEM((copies, 4 * slots.shape[0], tokens.shape[1] // 2), BF16),
            *(pltpu.VMEM(w.shape, BF16) for w in matrices),
        ),
        scratch_shapes=[
            pltpu.SMEM(slots.shape, slots.dtype),
            pltpu.SMEM(weights.shape, weights.dtype),
            pltpu.VMEM(tokens.shape, BF16),
            pltpu.VMEM(cotangent.shape, BF16),
            pltpu.SemaphoreType.DMA((6,)),
        ],
    )(slots, weights, tokens, cotangent, *matrices)


def on_chip(body, shape, dtype, *arrays):
    return pl.pallas_call(
        body, in_specs=[VMEM] * len(arrays), out_specs=VMEM, out_shape=pltpu.VMEM(shape, dtype)
    )(*(pltpu.with_memory_space_constraint(x, pltpu.VMEM) for x in arrays))


def pair(out, full, w_gate, w_up):
    groups, rows, d = out.shape
    return pl.pallas_call(
        slot_body,
        in_specs=[VMEM] * 4,
        out_specs=ANY,
        out_shape=jax.ShapeDtypeStruct((groups, 2, rows, d), BF16),
        scratch_shapes=[pltpu.VMEM(out.shape, BF16), pltpu.SemaphoreType.DMA((3,))],
    )(*(pltpu.with_memory_space_constraint(x, pltpu.VMEM) for x in (out, full, w_gate, w_up)))


def spots(slots, weights, tok):
    rows = 4 * slots.shape[0]
    return pl.pallas_call(
        spot_body,
        in_specs=[SMEM, SMEM],
        out_specs=(VMEM, VMEM),
        out_shape=(pltpu.VMEM((4 * tok, rows), BF16), pltpu.VMEM((rows, 128), F32)),
    )(slots, weights)


def place(hot, scale, pieces):
    out = jax.ShapeDtypeStruct((hot.shape[0] // 4, 2 * pieces.shape[2]), BF16)
    return pl.pallas_call(
        place_body,
        in_specs=[VMEM] * 3,
        out_specs=(ANY, ANY),
        out_shape=(out, out),
        scratch_shapes=[pltpu.VMEM(out.shape, BF16), pltpu.VMEM(out.shape, BF16), pltpu.SemaphoreType.DMA((2,))],
    )(*(pltpu.with_memory_space_constraint(x, pltpu.VMEM) for x in (hot, scale, pieces)))


def on_device(tokens, cotangent, w_gate, w_up, w_down, slot_token, route_weight):
    w_gate, w_up, w_down = w_gate[0], w_up[0], w_down[0]
    slots, weights = slot_token[0, 0], route_weight[0, 0]
    tok, d = tokens.shape
    cap = slots.shape[0]
    ff = w_gate.shape[1]

    half = ff // 2
    other = 1 - lax.axis_index("c").astype(jnp.uint32)
    sent_at = other * half
    kept_at = half - sent_at
    (near, w_gate, w_up), other, kept_at, sent_at = lax.optimization_barrier(
        (pick(slots, weights, tokens, cotangent, (w_gate, w_up), 8), other, kept_at, sent_at)
    )
    rows = exchange(on_chip(near_body, (8, 2, 8 * cap, d), BF16, exchange(near, "y")), ("zl", "x"))
    n = 64 * cap

    all_rows, all_grads = (rows[:, i].reshape(n, d) for i in range(2))
    part = jnp.stack([dot(w_gate, all_rows, 0, 1), dot(w_up, all_rows, 0, 1), dot(w_down, all_grads, 1, 1)])
    sent = lax.all_gather(lax.dynamic_slice_in_dim(part, sent_at, half, axis=1).astype(BF16), "c")
    sent = lax.dynamic_index_in_dim(sent, other, axis=0, keepdims=False)
    part = (lax.dynamic_slice_in_dim(part, kept_at, half, axis=1) + sent.astype(F32)).astype(BF16)
    part = part.reshape(3, 4, ff // 8, n).transpose(1, 0, 2, 3)
    gate_sum, up_sum, hidden_grad = total(exchange(part, "zh"))
    sigmoid_gate = jax.nn.sigmoid(gate_sum)
    activated = gate_sum * sigmoid_gate
    own = jnp.stack(
        [
            activated * up_sum,
            hidden_grad * up_sum * sigmoid_gate * (1.0 + gate_sum * (1.0 - sigmoid_gate)),
            hidden_grad * activated,
        ]
    ).astype(BF16)
    full = lax.all_gather(spread(own, "zh", 4), "c", axis=0, tiled=True)

    hidden, d_gate, d_up = (full[:, i].reshape(ff, n) for i in range(3))
    out = dot(hidden, w_down, 0, 0).astype(BF16)
    both = pair(out.reshape(8, 8 * cap, d), full, w_gate, w_up)
    both, slots, weights = lax.optimization_barrier((both, slots, weights))
    both = exchange(both, ("zl", "x"))

    grad_gate = dot(all_rows, d_gate, 0, 1).astype(BF16)
    grad_up = dot(all_rows, d_up, 0, 1).astype(BF16)
    grad_down = dot(hidden, all_grads, 1, 0).astype(BF16)
    both, grad_gate, grad_up, grad_down, (hot, scale) = lax.optimization_barrier(
        (both, grad_gate, grad_up, grad_down, spots(slots, weights, tok))
    )
    both = on_chip(regroup_body, (8, 4 * cap, d // 2), BF16, both)
    mixed, grad_tokens = place(hot, scale, exchange(both, "y"))
    return mixed, grad_tokens, grad_gate[None], grad_up[None], grad_down[None]


def solution(mesh):
    fine = Mesh(mesh.devices.reshape(SIZES), AXES)
    acts = P(DP, TENSOR)
    w_in = P(None, TENSOR, DP)
    w_out = P(None, DP, TENSOR)
    slot = P(DP, None, None)
    return jax.shard_map(
        on_device,
        mesh=fine,
        in_specs=(acts, acts, w_in, w_in, w_out, slot, slot),
        out_specs=(acts, acts, w_in, w_in, w_out),
        check_vma=False,
    )
```

```python
import jax
import jax.numpy as jnp
from jax import lax
from jax.experimental import pallas as pl
from jax.experimental.pallas import tpu as pltpu
from jax.sharding import Mesh
from jax.sharding import PartitionSpec as P

AXES = ("zl", "y", "x", "zh", "c")
SIZES = (2, 8, 4, 4, 2)
DP = ("zl", "y", "x")
TENSOR = ("zh", "c")
BF16 = jnp.bfloat16
F32 = jnp.float32


def exchange(pieces, axes):
    return lax.all_to_all(pieces, axes, split_axis=0, concat_axis=0, tiled=True)


def spread(piece, axes, n):
    return exchange(jnp.broadcast_to(piece[None], (n, *piece.shape)), axes)


def total(pieces):
    out = pieces[0].astype(F32)
    for j in range(1, pieces.shape[0]):
        out = out + pieces[j].astype(F32)
    return out


def dot(a, b, ca, cb):
    return lax.dot_general(a, b, (((ca,), (cb,)), ((), ())), preferred_element_type=F32)


def one_hot(slots_ref, shape, slot_dim, first):
    slot = lax.broadcasted_iota(jnp.int32, shape, slot_dim) - first
    token = lax.broadcasted_iota(jnp.int32, shape, 1 - slot_dim)
    wanted = jnp.full(shape, -1, jnp.int32)
    for s in range(slots_ref.shape[0]):
        wanted = jnp.where(slot == s, slots_ref[s], wanted)
    return (token == wanted).astype(F32).astype(BF16)


def by_slot(weights_ref, rows, first, other):
    slot = lax.broadcasted_iota(jnp.int32, (rows, 1), 0) - first
    out = jnp.full((rows, 1), other, F32)
    for s in range(weights_ref.shape[0]):
        out = jnp.where(slot == s, weights_ref[s], out)
    return out


def pick_body(*refs):
    sources, (out_ref, *matrix_refs, slots_ref, weights_ref, tokens_ref, cotangent_ref, sems) = refs[:6], refs[6:]
    targets = (slots_ref, weights_ref, tokens_ref, cotangent_ref, *matrix_refs)
    copies = [pltpu.make_async_copy(src, dst, sems.at[i]) for i, (src, dst) in enumerate(zip(sources, targets))]
    for copy in copies:
        copy.start()
    copies[0].wait()
    copies[1].wait()
    cap = slots_ref.shape[0]
    count, rows, half = out_ref.shape
    hots = [one_hot(slots_ref, (rows, tokens_ref.shape[0]), 0, k * cap) for k in range(4)]
    scale = by_slot(weights_ref, rows, cap, 0.0) + by_slot(weights_ref, rows, 3 * cap, 0.0)
    copies[2].wait()
    copies[3].wait()
    picked = dot(hots[0], tokens_ref[:, :half], 1, 0) + dot(hots[2], tokens_ref[:, half:], 1, 0)
    d_rows = dot(hots[1], cotangent_ref[:, :half], 1, 0) + dot(hots[3], cotangent_ref[:, half:], 1, 0)
    packed = (picked + scale * d_rows).astype(BF16)
    for j in range(count):
        out_ref[j] = packed
    for copy in copies[4:]:
        copy.wait()


def place_body(hot_ref, scale_ref, pieces_ref, *refs):
    half = pieces_ref.shape[2]
    tok = hot_ref.shape[0] // 4
    acc = pieces_ref[0].astype(F32)
    for j in range(1, pieces_ref.shape[0]):
        acc = acc + pieces_ref[j].astype(F32)
    acc = (acc * scale_ref[:, :1]).astype(BF16)
    sems = refs[4]
    copies = [pltpu.make_async_copy(refs[2 + k], refs[k], sems.at[k]) for k in range(2)]
    for k in range(2):
        for p in range(2):
            hot = hot_ref[(2 * p + k) * tok : (2 * p + k + 1) * tok]
            refs[2 + k][:, p * half : (p + 1) * half] = dot(hot, acc, 1, 0).astype(BF16)
        copies[k].start()
    for copy in copies:
        copy.wait()


def moves(blocks, cap, p):
    shape = (2 * blocks * cap, 4 * blocks * cap)
    row = lax.broadcasted_iota(jnp.int32, (shape[0], 1), 0)
    kind = (row >= blocks * cap).astype(jnp.int32)
    block = sum((row - kind * blocks * cap >= b * cap).astype(jnp.int32) for b in range(1, blocks))
    at = row + block * 3 * cap + 2 * p * cap + kind * (cap - blocks * cap)
    return (lax.broadcasted_iota(jnp.int32, shape, 1) == at).astype(F32).astype(BF16)


def near_body(pieces_ref, out_ref):
    blocks, rows, half = pieces_ref.shape
    count, _, kept, d = out_ref.shape
    pieces = pieces_ref[...].reshape(blocks * rows, half)
    both = [dot(moves(blocks, rows // 4, p), pieces, 1, 0).astype(BF16) for p in range(2)]
    both = jnp.concatenate(both, axis=1).reshape(2, kept, d)
    for j in range(count):
        out_ref[j] = both


def slot_body(out_ref, full_ref, w_gate_ref, w_up_ref, both_ref, back_ref, sems):
    copies = [pltpu.make_async_copy(out_ref, both_ref.at[:, 0], sems.at[0])]
    copies[0].start()
    groups, rows, d = out_ref.shape
    n = full_ref.shape[3]
    d_gate, d_up = (full_ref[:, i].reshape(-1, n).T for i in (1, 2))
    part = groups // 2
    for j in range(2):
        here = pl.ds(j * part, part)
        take = slice(j * part * rows, (j + 1) * part * rows)
        back = dot(d_gate[take], w_gate_ref[...], 1, 1) + dot(d_up[take], w_up_ref[...], 1, 1)
        back_ref[here] = back.astype(BF16).reshape(part, rows, d)
        copies.append(pltpu.make_async_copy(back_ref.at[here], both_ref.at[here, 1], sems.at[1 + j]))
        copies[-1].start()
    for copy in copies:
        copy.wait()


def spot_body(slots_ref, weights_ref, hot_ref, scale_ref):
    cap = slots_ref.shape[0]
    tok = hot_ref.shape[0] // 4
    for k in range(4):
        hot_ref[k * tok : (k + 1) * tok] = one_hot(slots_ref, (tok, 4 * cap), 1, k * cap)
    slot = lax.broadcasted_iota(jnp.int32, scale_ref.shape, 0)
    scale = jnp.ones(scale_ref.shape, F32)
    for s in range(cap):
        scale = jnp.where((slot == s) | (slot == 2 * cap + s), weights_ref[s], scale)
    scale_ref[...] = scale


def regroup_body(pieces_ref, out_ref):
    blocks, rows, half = out_ref.shape
    acc = pieces_ref[0].astype(F32)
    for j in range(1, pieces_ref.shape[0]):
        acc = acc + pieces_ref[j].astype(F32)
    acc = acc.reshape(-1, 2 * half).astype(BF16)
    out = sum(dot(moves(blocks, rows // 4, p), acc[:, p * half : (p + 1) * half], 0, 0) for p in range(2))
    out_ref[...] = out.astype(BF16).reshape(out_ref.shape)


SMEM = pl.BlockSpec(memory_space=pltpu.SMEM)
VMEM = pl.BlockSpec(memory_space=pltpu.VMEM)
ANY = pl.BlockSpec(memory_space=pl.ANY)


def pick(slots, weights, tokens, cotangent, matrices, copies):
    return pl.pallas_call(
        pick_body,
        in_specs=[ANY] * 6,
        out_specs=(VMEM, VMEM, VMEM),
        out_shape=(
            pltpu.VMEM((copies, 4 * slots.shape[0], tokens.shape[1] // 2), BF16),
            *(pltpu.VMEM(w.shape, BF16) for w in matrices),
        ),
        scratch_shapes=[
            pltpu.SMEM(slots.shape, slots.dtype),
            pltpu.SMEM(weights.shape, weights.dtype),
            pltpu.VMEM(tokens.shape, BF16),
            pltpu.VMEM(cotangent.shape, BF16),
            pltpu.SemaphoreType.DMA((6,)),
        ],
    )(slots, weights, tokens, cotangent, *matrices)


def on_chip(body, shape, dtype, *arrays):
    return pl.pallas_call(
        body, in_specs=[VMEM] * len(arrays), out_specs=VMEM, out_shape=pltpu.VMEM(shape, dtype)
    )(*(pltpu.with_memory_space_constraint(x, pltpu.VMEM) for x in arrays))


def pair(out, full, w_gate, w_up):
    groups, rows, d = out.shape
    return pl.pallas_call(
        slot_body,
        in_specs=[VMEM] * 4,
        out_specs=ANY,
        out_shape=jax.ShapeDtypeStruct((groups, 2, rows, d), BF16),
        scratch_shapes=[pltpu.VMEM(out.shape, BF16), pltpu.SemaphoreType.DMA((3,))],
    )(*(pltpu.with_memory_space_constraint(x, pltpu.VMEM) for x in (out, full, w_gate, w_up)))


def spots(slots, weights, tok):
    rows = 4 * slots.shape[0]
    return pl.pallas_call(
        spot_body,
        in_specs=[SMEM, SMEM],
        out_specs=(VMEM, VMEM),
        out_shape=(pltpu.VMEM((4 * tok, rows), BF16), pltpu.VMEM((rows, 128), F32)),
    )(slots, weights)


def place(hot, scale, pieces):
    out = jax.ShapeDtypeStruct((hot.shape[0] // 4, 2 * pieces.shape[2]), BF16)
    return pl.pallas_call(
        place_body,
        in_specs=[VMEM] * 3,
        out_specs=(ANY, ANY),
        out_shape=(out, out),
        scratch_shapes=[pltpu.VMEM(out.shape, BF16), pltpu.VMEM(out.shape, BF16), pltpu.SemaphoreType.DMA((2,))],
    )(*(pltpu.with_memory_space_constraint(x, pltpu.VMEM) for x in (hot, scale, pieces)))


def on_device(tokens, cotangent, w_gate, w_up, w_down, slot_token, route_weight):
    w_gate, w_up, w_down = w_gate[0], w_up[0], w_down[0]
    slots, weights = slot_token[0, 0], route_weight[0, 0]
    tok, d = tokens.shape
    cap = slots.shape[0]
    ff = w_gate.shape[1]

    half = ff // 2
    other = 1 - lax.axis_index("c").astype(jnp.uint32)
    sent_at = other * half
    kept_at = half - sent_at
    (near, w_gate, w_up), other, kept_at, sent_at = lax.optimization_barrier(
        (pick(slots, weights, tokens, cotangent, (w_gate, w_up), 8), other, kept_at, sent_at)
    )
    rows = exchange(on_chip(near_body, (8, 2, 8 * cap, d), BF16, exchange(near, "y")), ("x", "zl"))
    n = 64 * cap

    all_rows, all_grads = (rows[:, i].reshape(n, d) for i in range(2))
    part = jnp.stack([dot(w_gate, all_rows, 0, 1), dot(w_up, all_rows, 0, 1), dot(w_down, all_grads, 1, 1)])
    sent = lax.all_gather(lax.dynamic_slice_in_dim(part, sent_at, half, axis=1).astype(BF16), "c")
    sent = lax.dynamic_index_in_dim(sent, other, axis=0, keepdims=False)
    part = (lax.dynamic_slice_in_dim(part, kept_at, half, axis=1) + sent.astype(F32)).astype(BF16)
    part = part.reshape(3, 4, ff // 8, n).transpose(1, 0, 2, 3)
    gate_sum, up_sum, hidden_grad = total(exchange(part, "zh"))
    sigmoid_gate = jax.nn.sigmoid(gate_sum)
    activated = gate_sum * sigmoid_gate
    own = jnp.stack(
        [
            activated * up_sum,
            hidden_grad * up_sum * sigmoid_gate * (1.0 + gate_sum * (1.0 - sigmoid_gate)),
            hidden_grad * activated,
        ]
    ).astype(BF16)
    full = lax.all_gather(spread(own, "zh", 4), "c", axis=0, tiled=True)

    hidden, d_gate, d_up = (full[:, i].reshape(ff, n) for i in range(3))
    out = dot(hidden, w_down, 0, 0).astype(BF16)
    both = pair(out.reshape(8, 8 * cap, d), full, w_gate, w_up)
    both, slots, weights = lax.optimization_barrier((both, slots, weights))
    both = exchange(both, ("x", "zl"))

    grad_gate = dot(all_rows, d_gate, 0, 1).astype(BF16)
    grad_up = dot(all_rows, d_up, 0, 1).astype(BF16)
    grad_down = dot(hidden, all_grads, 1, 0).astype(BF16)
    both, grad_gate, grad_up, grad_down, (hot, scale) = lax.optimization_barrier(
        (both, grad_gate, grad_up, grad_down, spots(slots, weights, tok))
    )
    both = on_chip(regroup_body, (8, 4 * cap, d // 2), BF16, both)
    mixed, grad_tokens = place(hot, scale, exchange(both, "y"))
    return mixed, grad_tokens, grad_gate[None], grad_up[None], grad_down[None]


def solution(mesh):
    fine = Mesh(mesh.devices.reshape(SIZES), AXES)
    acts = P(DP, TENSOR)
    w_in = P(None, TENSOR, DP)
    w_out = P(None, DP, TENSOR)
    slot = P(DP, None, None)
    return jax.shard_map(
        on_device,
        mesh=fine,
        in_specs=(acts, acts, w_in, w_in, w_out, slot, slot),
        out_specs=(acts, acts, w_in, w_in, w_out),
        check_vma=False,
    )
```
